32 devices in a mesh: group: 8 (over z, x), inner: 4 (over y, core).
Axes of the slice: x: 2, y: 2, z: 4, core: 2. Of those that a mesh axis runs over, the one named last changes fastest.
Arguments:
- state: float32 [2, 4194304], P(None, ('group', 'inner')), may hold values from -6 to 6
- gates: float32 [8, 2, 128, 128], replicated, may hold values from -0.375 to 0.375
Outputs:
- evolved: float32 [2, 4194304], P(None, ('group', 'inner'))
The draws below stay inside these ranges and needn't reach their ends.
All inputs are finite; a program needn't handle non-finite values.
Results may differ from the reference program's by a relative error of at most 0.000073.
Values sent between devices are 32-bit elements; how exact they have to be, the bound alone decides.
A program may use at most 64 MiB of HBM per device.

```python
import jax
import jax.numpy as jnp
from jax import lax

GQ = 7
GDIM = 128
LOCQ = 17
NGATES = 8
AMP_DEV = 131072
AMPS = 4194304
N_GROUP = 8
N_INNER = 4


def block_levels(stream_key, extent, cuts, least, largest):
    factor_of, own = 1.0, jax.random.fold_in(stream_key, 6)
    for position, parts in cuts:
        heights = jnp.exp(jax.random.uniform(jax.random.fold_in(own, position), (parts,), jnp.float32, least / len(cuts), largest / len(cuts)))
        factor_of = factor_of * jnp.repeat(heights, extent[position] // parts).reshape([-1 if axis == position else 1 for axis in range(len(extent))])
    return factor_of


def scatter_about(own_key, extent, spread, bound, split=(), kind=jnp.bfloat16):
    level = block_levels(own_key, extent, split, -0.22, 0.18) if split else 1.0
    values = jax.random.normal(own_key, extent, jnp.float32) * spread * level
    return jnp.minimum(jnp.maximum(values, -bound), bound).astype(kind)


def setup_inputs(seed: int = 0) -> dict:
    keys = jax.random.split(jax.random.key(seed), 3)
    return {
        "state": scatter_about(keys[0], (2, AMPS), 1.0, 6.0, ((1, 32),), jnp.float32),
        "gates": scatter_about(keys[1], (NGATES, 2, GDIM, GDIM), (2 * GDIM) ** -0.5, 0.375, (), jnp.float32),
    }


def apply_gate(state, mixer, start):
    size = mixer.shape[-1]
    total = state.shape[1]
    real_part = mixer[0]
    imag_part = mixer[1]
    block = jnp.stack([jnp.stack([real_part, -imag_part], 1), jnp.stack([imag_part, real_part], 1)], 0)
    if start == 0:
        view = state.reshape(2, total // size, size)
        result = jnp.einsum("ckdj,daj->cak", block, view, precision=lax.Precision.HIGHEST)
    else:
        view = state.reshape(2, total // (size << start), size, 1 << start)
        result = jnp.einsum("ckdj,dajb->cakb", block, view, precision=lax.Precision.HIGHEST)
    return result.reshape(2, total)


def swap_middle(whole):
    shaped = whole.reshape(2, N_GROUP, N_INNER, N_INNER, AMP_DEV // N_INNER)
    return jnp.transpose(shaped, (0, 1, 3, 2, 4)).reshape(2, -1)


def swap_top(whole):
    shaped = whole.reshape(2, N_GROUP, N_INNER, N_INNER, N_GROUP, AMP_DEV // (N_INNER * N_GROUP))
    return jnp.transpose(shaped, (0, 4, 2, 3, 1, 5)).reshape(2, -1)


def reference(state, gates):
    inner_bits = N_INNER.bit_length() - 1
    upper = LOCQ - GQ
    whole = apply_gate(state, gates[0], 0)
    whole = apply_gate(whole, gates[1], upper)
    whole = swap_middle(whole)
    whole = apply_gate(whole, gates[3], 0)
    whole = apply_gate(whole, gates[2], upper)
    whole = swap_top(whole)
    whole = apply_gate(whole, gates[4], upper - inner_bits)
    whole = apply_gate(whole, gates[5], 0)
    whole = apply_gate(whole, gates[6], upper)
    whole = apply_gate(whole, gates[7], upper // 2)
    whole = swap_top(whole)
    whole = swap_middle(whole)
    return whole
```

```python
import functools

import jax
import jax.numpy as jnp
from jax import lax
from jax.experimental import pallas as pl
from jax.experimental.pallas import tpu as pltpu
from jax.sharding import PartitionSpec as P


def blocked(mixer):
    real_part = mixer[0]
    imag_part = mixer[1]
    return jnp.stack(
        [jnp.stack([real_part, -imag_part], 1), jnp.stack([imag_part, real_part], 1)], 0
    )


def apply_gate(state, mixer, start):
    size = mixer.shape[-1]
    total = state.shape[1]
    block = blocked(mixer)
    if start == 0:
        view = state.reshape(2, total // size, size)
        result = jnp.einsum("ckdj,daj->cak", block, view, precision=lax.Precision.HIGHEST)
    else:
        view = state.reshape(2, total // (size << start), size, 1 << start)
        result = jnp.einsum("ckdj,dajb->cakb", block, view, precision=lax.Precision.HIGHEST)
    return result.reshape(2, total)


def general_body(state, gates):
    n_inner = lax.axis_size("inner")
    n_group = lax.axis_size("group")
    total = state.shape[1]
    size = gates.shape[-1]
    local_bits = total.bit_length() - 1
    gate_bits = size.bit_length() - 1
    inner_bits = n_inner.bit_length() - 1
    upper = local_bits - gate_bits
    amps = apply_gate(state, gates[0], 0)
    amps = apply_gate(amps, gates[1], upper)
    low_gate = gates[3]
    shaped = amps.reshape(2, n_inner, total // (n_inner * size), size)
    pieces = lax.all_to_all(shaped, "inner", split_axis=1, concat_axis=1, tiled=True)
    amps = apply_gate(pieces.reshape(2, -1), low_gate, 0).reshape(pieces.shape).reshape(2, total)
    amps = apply_gate(amps, gates[2], upper)
    shaped = amps.reshape(2, n_inner, n_group, total // (n_inner * n_group))
    amps = lax.all_to_all(shaped, "group", split_axis=2, concat_axis=2, tiled=True).reshape(
        2, total
    )
    amps = apply_gate(amps, gates[4], upper - inner_bits)
    amps = apply_gate(amps, gates[5], 0)
    amps = apply_gate(amps, gates[6], upper)
    amps = apply_gate(amps, gates[7], upper // 2)
    shaped = amps.reshape(2, n_inner, n_group, total // (n_inner * n_group))
    shaped = lax.all_to_all(shaped, "group", split_axis=2, concat_axis=2, tiled=True)
    shaped = lax.all_to_all(shaped, "inner", split_axis=1, concat_axis=1, tiled=True)
    return shaped.reshape(2, total)


F32 = jnp.float32
BF16 = jnp.bfloat16


def split(value):
    high = value.astype(BF16)
    return high, (value - high.astype(F32)).astype(BF16)


def dot3(left, right, transposed=False):
    dims = (((1,), (1 if transposed else 0,)), ((), ()))
    mul = functools.partial(lax.dot_general, dimension_numbers=dims, preferred_element_type=F32)
    (lh, ll), (rh, rl) = left, right
    return mul(lh, rh) + (mul(lh, rl) + mul(ll, rh))


def exchange(x, axis, pairs):
    lane = lax.broadcasted_iota(jnp.int32, (1, x.shape[-1]), 1)
    for lane_bit, bit in pairs:
        shift = 1 << lane_bit
        upper = ((lane >> lane_bit) & 1) == 1
        shape = x.shape
        y = x.reshape(shape[:axis] + (shape[axis] >> (bit + 1), 2, 1 << bit) + shape[axis + 1 :])
        cut = (slice(None),) * (axis + 1)
        a, b = y[cut + (0,)], y[cut + (1,)]
        rows = a.reshape(-1, shape[-1])
        ra = pltpu.roll(rows, shape[-1] - shift, 1).reshape(a.shape)
        rb = pltpu.roll(b.reshape(-1, shape[-1]), shift, 1).reshape(a.shape)
        first = jnp.where(upper, rb, a)
        second = jnp.where(upper, b, ra)
        x = jnp.stack([first, second], axis + 1).reshape(shape)
    return x


def kernel(
    n_group, n_inner, x_ref, w_ref, o_ref, send1, recv1, send2, recv2, tmp, weights, ssem, rsem
):
    devices = n_group * n_inner
    size = x_ref.shape[1]
    wide = 2 * size
    mid = x_ref.shape[0] // wide
    rest = size // devices
    low = size // devices
    half = size // n_group // low
    seven = mid // half
    chunks = 2
    sub = 2 * low
    group, inner = lax.axis_index("group"), lax.axis_index("inner")
    me = group * n_inner + inner

    def peer(step):
        other = lax.rem(me + step, devices)
        return other, (other // n_inner, lax.rem(other, n_inner))

    barrier = pltpu.get_barrier_semaphore()

    @pl.loop(1, devices)
    def _(step):
        pl.semaphore_signal(
            barrier, inc=1, device_id=peer(step)[1], device_id_type=pl.DeviceIdType.MESH
        )

    for k in range(w_ref.shape[0]):
        weights[k, 0], weights[k, 1] = split(w_ref[k])

    def weight(k):
        return weights[k, 0], weights[k, 1]

    def copies(swap, chunk, step, source, landing):
        other, where = peer(step)
        return pltpu.make_async_remote_copy(
            src_ref=source.at[chunk, other],
            dst_ref=landing.at[chunk, me],
            send_sem=ssem.at[swap, chunk, step],
            recv_sem=rsem.at[swap, chunk, step],
            device_id=where,
            device_id_type=pl.DeviceIdType.MESH,
        )

    def start(swap, chunk, source, landing):
        @pl.loop(1, devices)
        def _(step):
            copies(swap, chunk, step, source, landing).start()

        landing[chunk, me] = source[chunk, me]

    def finish(swap, chunk, source, landing):
        @pl.loop(1, devices)
        def _(step):
            copies(swap, chunk, step, source, landing).wait()

    cols = [
        jnp.concatenate(
            [x_ref[pl.ds(2 * q + c, size, stride=2 * mid), :] for c in range(2)], axis=0
        )
        for q in range(mid)
    ]
    y = dot3(weight(0), split(jnp.concatenate(cols, axis=1)))
    run = size // (chunks * low)
    tiles = [
        y[:, q * size : (q + 1) * size].reshape(2, chunks, low, run, size) for q in range(mid)
    ]
    y = jnp.stack(tiles, 3)
    y = y.reshape(2, chunks, low * size, size)
    pl.semaphore_wait(barrier, devices - 1)
    for chunk in range(chunks):
        rows = jnp.concatenate([y[0, chunk], y[1, chunk]], axis=1)
        z = dot3(weight(1), split(rows), True)
        for w in range(low):
            piece = z[:, w * size : (w + 1) * size].reshape(devices, 2 * rest, size)
            send1[chunk, :, w * 2 * rest : (w + 1) * 2 * rest, :] = piece
        start(0, chunk, send1, recv1)

    bits_t = range(n_group.bit_length() - 1)
    lane_bits = size.bit_length() - 1
    bits_r = range(rest.bit_length() - 1)
    top = lane_bits - len(bits_r)
    pair_tu = [(k, k) for k in bits_t]
    pair_er = [(top + k, k) for k in bits_r]
    pair_t7 = [(lane_bits - len(bits_t) + k, k) for k in bits_t]

    def apply(k, x, axis):
        parts = x.shape[axis]
        picked = [lax.index_in_dim(x, i, axis, keepdims=False) for i in range(parts)]
        kept = picked[0].shape
        flat = jnp.concatenate([p.reshape(wide, size) for p in picked], axis=1)
        out = dot3(weight(k), split(flat))
        pieces = [out[:, i * size : (i + 1) * size].reshape(kept) for i in range(parts)]
        return jnp.stack(pieces, axis)

    for chunk in range(chunks):
        finish(0, chunk, send1, recv1)
        flat = recv1.at[chunk].reshape(devices * sub * rest, size)
        x = jnp.stack([flat[pl.ds(r, devices * sub, stride=rest), :] for r in range(rest)], 0)
        x = x.reshape(rest, n_group, n_inner, sub, size)
        x = exchange(x, 1, pair_tu)
        x = apply(2, x, 0)
        x = exchange(x, 1, pair_tu)
        x = exchange(x, 0, pair_er)
        x = apply(3, x, 2)
        x = apply(4, x, 0)
        x = exchange(x, 1, pair_t7)
        x = apply(5, x, 2)
        x = exchange(x, 1, pair_t7)
        x = x.reshape(half, devices, sub, size)
        for e in range(half):
            send2[chunk, :, e * sub : (e + 1) * sub, :] = x[e]
        start(1, chunk, send2, recv2)

    span = x_ref.shape[0] // chunks
    for chunk in range(chunks):
        finish(1, chunk, send2, recv2)
        x = recv2[chunk].reshape(devices, half, sub, size)
        x = exchange(x, 0, [(k, k) for k in range(top)])
        x = x.reshape(seven, devices // seven, half, sub, size)
        for p in range(seven):
            for e in range(half):
                tmp[:, (e * seven + p) * sub : (e * seven + p + 1) * sub, :] = x[p, :, e]
        flat = tmp.reshape(devices // seven * mid * sub, size)
        for hi in range(devices // seven):
            for w in range(low):
                for c in range(2):
                    rows = flat[pl.ds(hi * mid * sub + w * 2 + c, mid, stride=sub), :]
                    at = chunk * span + (hi * low + w) * 2 * mid + c
                    o_ref[pl.ds(at, mid, stride=2), :] = rows


def square(mixer, dims, order, columns=True):
    count = len(dims)
    block = blocked(mixer).reshape((2,) + dims + (2,) + dims)
    perm = tuple(k + 1 for k in order)
    second = tuple(k + 1 + count for k in perm) if columns else tuple(range(count + 1, 2 * count + 2))
    wide = 2 * mixer.shape[-1]
    return block.transpose(perm + second).reshape(wide, wide)


def fast_body(state, gates, n_group, n_inner):
    size = gates.shape[-1]
    total = state.shape[1]
    devices = n_group * n_inner
    rest = low = size // devices
    half = size // n_group // low
    mid = total // size // size
    seven = mid // half
    mul = functools.partial(jnp.matmul, precision=lax.Precision.HIGHEST)
    wide = 2 * size
    merged = mul(
        blocked(gates[5]).reshape(wide, wide),
        mul(blocked(gates[3]).reshape(wide, wide), blocked(gates[0]).reshape(wide, wide)),
    )
    merged = merged.reshape(2, rest, devices, wide).transpose(2, 0, 1, 3).reshape(wide, wide)
    w = jnp.stack(
        [
            square(gates[1], (2, n_inner // 2, n_group, low), (-1, 0, 3, 1, 2), False),
            merged,
            square(gates[2], (n_inner, n_group, low), (1, 0, 2, -1)),
            square(gates[4], (n_group, low, half), (2, 0, 1, -1)),
            square(gates[6], (n_inner, n_group, low), (1, 0, 2, -1)),
            square(gates[7], (low, half, seven, rest), (1, 3, 2, 0, -1)),
        ]
    )
    x = state.reshape(2, total // size, size).transpose(1, 0, 2).reshape(-1, size)
    chunk = (2, devices, x.shape[0] // 2 // devices, size)
    vmem = pl.BlockSpec(memory_space=pltpu.VMEM)
    out = pl.pallas_call(
        functools.partial(kernel, n_group, n_inner),
        out_shape=jax.ShapeDtypeStruct(x.shape, F32),
        in_specs=[vmem, vmem],
        out_specs=vmem,
        scratch_shapes=[
            pltpu.VMEM(chunk, F32),
            pltpu.VMEM(chunk, F32),
            pltpu.VMEM(chunk, F32),
            pltpu.VMEM(chunk, F32),
            pltpu.VMEM((devices // seven, mid * 2 * low, size), F32),
            pltpu.VMEM((w.shape[0], 2, wide, wide), BF16),
            pltpu.SemaphoreType.DMA((2, 2, devices)),
            pltpu.SemaphoreType.DMA((2, 2, devices)),
        ],
        compiler_params=pltpu.CompilerParams(
            collective_id=0, has_side_effects=True, vmem_limit_bytes=40 << 20
        ),
    )(x, w)
    return out.reshape(total // size, 2, size).transpose(1, 0, 2).reshape(2, total)


def solution(mesh):
    n_inner, n_group = mesh.shape["inner"], mesh.shape["group"]

    def body(state, gates):
        size, total = gates.shape[-1], state.shape[1]
        gate_bits, local_bits = size.bit_length() - 1, total.bit_length() - 1
        inner_bits = n_inner.bit_length() - 1
        device_bits = inner_bits + n_group.bit_length() - 1
        upper = local_bits - gate_bits
        fits = (
            device_bits == upper // 2
            and upper // 2 + gate_bits == local_bits - device_bits
            and upper - inner_bits >= gate_bits
        )
        if fits:
            return fast_body(state, gates, n_group, n_inner)
        return general_body(state, gates)

    in_specs = (P(None, ("group", "inner")), P())
    out_specs = P(None, ("group", "inner"))
    return jax.shard_map(body, mesh=mesh, in_specs=in_specs, out_specs=out_specs, check_vma=False)
```

```python
import functools

import jax
import jax.numpy as jnp
from jax import lax
from jax.experimental import pallas as pl
from jax.experimental.pallas import tpu as pltpu
from jax.sharding import PartitionSpec as P


def blocked(mixer):
    real_part = mixer[0]
    imag_part = mixer[1]
    return jnp.stack(
        [jnp.stack([real_part, -imag_part], 1), jnp.stack([imag_part, real_part], 1)], 0
    )


def apply_gate(state, mixer, start):
    size = mixer.shape[-1]
    total = state.shape[1]
    block = blocked(mixer)
    if start == 0:
        view = state.reshape(2, total // size, size)
        result = jnp.einsum("ckdj,daj->cak", block, view, precision=lax.Precision.HIGHEST)
    else:
        view = state.reshape(2, total // (size << start), size, 1 << start)
        result = jnp.einsum("ckdj,dajb->cakb", block, view, precision=lax.Precision.HIGHEST)
    return result.reshape(2, total)


def general_body(state, gates):
    n_inner = lax.axis_size("inner")
    n_group = lax.axis_size("group")
    total = state.shape[1]
    size = gates.shape[-1]
    local_bits = total.bit_length() - 1
    gate_bits = size.bit_length() - 1
    inner_bits = n_inner.bit_length() - 1
    upper = local_bits - gate_bits
    amps = apply_gate(state, gates[0], 0)
    amps = apply_gate(amps, gates[1], upper)
    low_gate = gates[3]
    shaped = amps.reshape(2, n_inner, total // (n_inner * size), size)
    pieces = lax.all_to_all(shaped, "inner", split_axis=1, concat_axis=1, tiled=True)
    amps = apply_gate(pieces.reshape(2, -1), low_gate, 0).reshape(pieces.shape).reshape(2, total)
    amps = apply_gate(amps, gates[2], upper)
    shaped = amps.reshape(2, n_inner, n_group, total // (n_inner * n_group))
    amps = lax.all_to_all(shaped, "group", split_axis=2, concat_axis=2, tiled=True).reshape(
        2, total
    )
    amps = apply_gate(amps, gates[4], upper - inner_bits)
    amps = apply_gate(amps, gates[5], 0)
    amps = apply_gate(amps, gates[6], upper)
    amps = apply_gate(amps, gates[7], upper // 2)
    shaped = amps.reshape(2, n_inner, n_group, total // (n_inner * n_group))
    shaped = lax.all_to_all(shaped, "group", split_axis=2, concat_axis=2, tiled=True)
    shaped = lax.all_to_all(shaped, "inner", split_axis=1, concat_axis=1, tiled=True)
    return shaped.reshape(2, total)


F32 = jnp.float32
BF16 = jnp.bfloat16


def split(value):
    high = value.astype(BF16)
    return high, (value - high.astype(F32)).astype(BF16)


def dot3(left, right, transposed=False):
    dims = (((1,), (1 if transposed else 0,)), ((), ()))
    mul = functools.partial(lax.dot_general, dimension_numbers=dims, preferred_element_type=F32)
    (lh, ll), (rh, rl) = left, right
    return mul(lh, rh) + (mul(lh, rl) + mul(ll, rh))


def exchange(x, axis, pairs):
    lane = lax.broadcasted_iota(jnp.int32, (1, x.shape[-1]), 1)
    for lane_bit, bit in pairs:
        shift = 1 << lane_bit
        upper = ((lane >> lane_bit) & 1) == 1
        shape = x.shape
        y = x.reshape(shape[:axis] + (shape[axis] >> (bit + 1), 2, 1 << bit) + shape[axis + 1 :])
        cut = (slice(None),) * (axis + 1)
        a, b = y[cut + (0,)], y[cut + (1,)]
        rows = a.reshape(-1, shape[-1])
        ra = pltpu.roll(rows, shape[-1] - shift, 1).reshape(a.shape)
        rb = pltpu.roll(b.reshape(-1, shape[-1]), shift, 1).reshape(a.shape)
        first = jnp.where(upper, rb, a)
        second = jnp.where(upper, b, ra)
        x = jnp.stack([first, second], axis + 1).reshape(shape)
    return x


def order_index(index, dims, order):
    bits = [d.bit_length() - 1 for d in dims]
    source, low = 0, 0
    for axis in reversed(order):
        digit = (index >> low) & (dims[axis] - 1)
        source = source + (digit << sum(bits[axis + 1 :]))
        low += bits[axis]
    return source


def kernel(
    n_group, n_inner, x_ref, g_ref, o_ref, send1, recv1, send2, recv2, tmp, weights, ssem, rsem
):
    devices = n_group * n_inner
    size = x_ref.shape[1]
    wide = 2 * size
    mid = x_ref.shape[0] // wide
    rest = size // devices
    low = size // devices
    half = size // n_group // low
    seven = mid // half
    chunks = 2
    sub = 2 * low
    group, inner = lax.axis_index("group"), lax.axis_index("inner")
    me = group * n_inner + inner

    def peer(step):
        other = lax.rem(me + step, devices)
        return other, (other // n_inner, lax.rem(other, n_inner))

    barrier = pltpu.get_barrier_semaphore()

    @pl.loop(1, devices)
    def _(step):
        pl.semaphore_signal(
            barrier, inc=1, device_id=peer(step)[1], device_id_type=pl.DeviceIdType.MESH
        )

    def gate(k):
        re, im = g_ref[k, 0], g_ref[k, 1]
        return jnp.concatenate(
            [jnp.concatenate([re, -im], axis=1), jnp.concatenate([im, re], axis=1)], axis=0
        )

    def place(k, matrix, order, columns=True):
        for part, piece in enumerate(split(matrix)):
            piece = select(order, piece)
            if columns:
                piece = select(order, piece, False)
            weights[k, part] = piece.astype(BF16)

    def select(order, piece, rows=True):
        shape = (wide, wide)
        source = order_index(lax.broadcasted_iota(jnp.int32, shape, 0), *order)
        hit = source == lax.broadcasted_iota(jnp.int32, shape, 1)
        ones = jnp.where(hit, 1.0, 0.0).astype(BF16)
        left, right = (ones, piece) if rows else (piece.astype(BF16), ones)
        dims = (((1,), (0 if rows else 1,)), ((), ()))
        return lax.dot_general(left, right, dims, preferred_element_type=F32)

    def weight(k):
        return weights[k, 0], weights[k, 1]

    def copies(swap, chunk, step, source, landing):
        other, where = peer(step)
        return pltpu.make_async_remote_copy(
            src_ref=source.at[chunk, other],
            dst_ref=landing.at[chunk, me],
            send_sem=ssem.at[swap, chunk, step],
            recv_sem=rsem.at[swap, chunk, step],
            device_id=where,
            device_id_type=pl.DeviceIdType.MESH,
        )

    def start(swap, chunk, source, landing):
        @pl.loop(1, devices)
        def _(step):
            copies(swap, chunk, step, source, landing).start()

        landing[chunk, me] = source[chunk, me]

    def finish(swap, chunk, source, landing):
        @pl.loop(1, devices)
        def _(step):
            copies(swap, chunk, step, source, landing).wait()

    place(0, gate(1), ((2, chunks, n_inner // chunks, n_group, low), (0, 1, 4, 2, 3)), False)
    merged = dot3(split(gate(3)), split(gate(0)))
    merged = dot3(split(gate(5)), split(merged))
    place(1, merged, ((2, rest, devices), (2, 0, 1)), False)

    cols = [
        jnp.concatenate(
            [x_ref[pl.ds(2 * q + c, size, stride=2 * mid), :] for c in range(2)], axis=0
        )
        for q in range(mid)
    ]
    y = dot3(weight(0), split(jnp.concatenate(cols, axis=1)))
    run = size // (chunks * low)
    tiles = [
        y[:, q * size : (q + 1) * size].reshape(2, chunks, low, run, size) for q in range(mid)
    ]
    y = jnp.stack(tiles, 3)
    y = y.reshape(2, chunks, low * size, size)
    pl.semaphore_wait(barrier, devices - 1)
    for chunk in range(chunks):
        rows = jnp.concatenate([y[0, chunk], y[1, chunk]], axis=1)
        z = dot3(weight(1), split(rows), True)
        for w in range(low):
            piece = z[:, w * size : (w + 1) * size].reshape(devices, 2 * rest, size)
            send1[chunk, :, w * 2 * rest : (w + 1) * 2 * rest, :] = piece
        start(0, chunk, send1, recv1)

    place(2, gate(2), ((2, n_inner, n_group, low), (2, 1, 3, 0)))
    place(3, gate(4), ((2, n_group, low, half), (3, 1, 2, 0)))
    place(4, gate(6), ((2, n_inner, n_group, low), (2, 1, 3, 0)))
    place(5, gate(7), ((2, low, half, seven, rest), (2, 4, 3, 1, 0)))

    bits_t = range(n_group.bit_length() - 1)
    lane_bits = size.bit_length() - 1
    bits_r = range(rest.bit_length() - 1)
    top = lane_bits - len(bits_r)
    pair_tu = [(k, k) for k in bits_t]
    pair_er = [(top + k, k) for k in bits_r]
    pair_t7 = [(lane_bits - len(bits_t) + k, k) for k in bits_t]

    def apply(k, x, axis):
        parts = x.shape[axis]
        picked = [lax.index_in_dim(x, i, axis, keepdims=False) for i in range(parts)]
        kept = picked[0].shape
        flat = jnp.concatenate([p.reshape(wide, size) for p in picked], axis=1)
        out = dot3(weight(k), split(flat))
        pieces = [out[:, i * size : (i + 1) * size].reshape(kept) for i in range(parts)]
        return jnp.stack(pieces, axis)

    for chunk in range(chunks):
        finish(0, chunk, send1, recv1)
        flat = recv1.at[chunk].reshape(devices * sub * rest, size)
        x = jnp.stack([flat[pl.ds(r, devices * sub, stride=rest), :] for r in range(rest)], 0)
        x = x.reshape(rest, n_group, n_inner, sub, size)
        x = exchange(x, 1, pair_tu)
        x = apply(2, x, 0)
        x = exchange(x, 1, pair_tu)
        x = exchange(x, 0, pair_er)
        x = apply(3, x, 2)
        x = apply(4, x, 0)
        x = exchange(x, 1, pair_t7)
        x = apply(5, x, 2)
        x = exchange(x, 1, pair_t7)
        x = x.reshape(half, devices, sub, size)
        for e in range(half):
            send2[chunk, :, e * sub : (e + 1) * sub, :] = x[e]
        start(1, chunk, send2, recv2)

    span = x_ref.shape[0] // chunks
    for chunk in range(chunks):
        finish(1, chunk, send2, recv2)
        x = recv2[chunk].reshape(devices, half, sub, size)
        x = exchange(x, 0, [(k, k) for k in range(top)])
        x = x.reshape(seven, devices // seven, half, sub, size)
        for p in range(seven):
            for e in range(half):
                tmp[:, (e * seven + p) * sub : (e * seven + p + 1) * sub, :] = x[p, :, e]
        flat = tmp.reshape(devices // seven * mid * sub, size)
        for hi in range(devices // seven):
            for w in range(low):
                for c in range(2):
                    rows = flat[pl.ds(hi * mid * sub + w * 2 + c, mid, stride=sub), :]
                    at = chunk * span + (hi * low + w) * 2 * mid + c
                    o_ref[pl.ds(at, mid, stride=2), :] = rows


def fast_body(state, gates, n_group, n_inner):
    size = gates.shape[-1]
    total = state.shape[1]
    devices = n_group * n_inner
    low = size // devices
    half = size // n_group // low
    mid = total // size // size
    seven = mid // half
    wide = 2 * size
    x = state.reshape(2, total // size, size).transpose(1, 0, 2).reshape(-1, size)
    chunk = (2, devices, x.shape[0] // 2 // devices, size)
    vmem = pl.BlockSpec(memory_space=pltpu.VMEM)
    out = pl.pallas_call(
        functools.partial(kernel, n_group, n_inner),
        out_shape=jax.ShapeDtypeStruct(x.shape, F32),
        in_specs=[vmem, vmem],
        out_specs=vmem,
        scratch_shapes=[
            pltpu.VMEM(chunk, F32),
            pltpu.VMEM(chunk, F32),
            pltpu.VMEM(chunk, F32),
            pltpu.VMEM(chunk, F32),
            pltpu.VMEM((devices // seven, mid * 2 * low, size), F32),
            pltpu.VMEM((6, 2, wide, wide), BF16),
            pltpu.SemaphoreType.DMA((2, 2, devices)),
            pltpu.SemaphoreType.DMA((2, 2, devices)),
        ],
        compiler_params=pltpu.CompilerParams(
            collective_id=0, has_side_effects=True, vmem_limit_bytes=40 << 20
        ),
    )(x, gates)
    return out.reshape(total // size, 2, size).transpose(1, 0, 2).reshape(2, total)


def solution(mesh):
    n_inner, n_group = mesh.shape["inner"], mesh.shape["group"]

    def body(state, gates):
        size, total = gates.shape[-1], state.shape[1]
        gate_bits, local_bits = size.bit_length() - 1, total.bit_length() - 1
        inner_bits = n_inner.bit_length() - 1
        device_bits = inner_bits + n_group.bit_length() - 1
        upper = local_bits - gate_bits
        fits = (
            device_bits == upper // 2
            and upper // 2 + gate_bits == local_bits - device_bits
            and upper - inner_bits >= gate_bits
        )
        if fits:
            return fast_body(state, gates, n_group, n_inner)
        return general_body(state, gates)

    in_specs = (P(None, ("group", "inner")), P())
    out_specs = P(None, ("group", "inner"))
    return jax.shard_map(body, mesh=mesh, in_specs=in_specs, out_specs=out_specs, check_vma=False)
```

```python
import functools

import jax
import jax.numpy as jnp
from jax import lax
from jax.experimental import pallas as pl
from jax.experimental.pallas import tpu as pltpu
from jax.sharding import PartitionSpec as P


def blocked(mixer):
    real_part = mixer[0]
    imag_part = mixer[1]
    return jnp.stack(
        [jnp.stack([real_part, -imag_part], 1), jnp.stack([imag_part, real_part], 1)], 0
    )


def apply_gate(state, mixer, start):
    size = mixer.shape[-1]
    total = state.shape[1]
    block = blocked(mixer)
    if start == 0:
        view = state.reshape(2, total // size, size)
        result = jnp.einsum("ckdj,daj->cak", block, view, precision=lax.Precision.HIGHEST)
    else:
        view = state.reshape(2, total // (size << start), size, 1 << start)
        result = jnp.einsum("ckdj,dajb->cakb", block, view, precision=lax.Precision.HIGHEST)
    return result.reshape(2, total)


def general_body(state, gates):
    n_inner = lax.axis_size("inner")
    n_group = lax.axis_size("group")
    total = state.shape[1]
    size = gates.shape[-1]
    local_bits = total.bit_length() - 1
    gate_bits = size.bit_length() - 1
    inner_bits = n_inner.bit_length() - 1
    upper = local_bits - gate_bits
    amps = apply_gate(state, gates[0], 0)
    amps = apply_gate(amps, gates[1], upper)
    low_gate = gates[3]
    shaped = amps.reshape(2, n_inner, total // (n_inner * size), size)
    pieces = lax.all_to_all(shaped, "inner", split_axis=1, concat_axis=1, tiled=True)
    amps = apply_gate(pieces.reshape(2, -1), low_gate, 0).reshape(pieces.shape).reshape(2, total)
    amps = apply_gate(amps, gates[2], upper)
    shaped = amps.reshape(2, n_inner, n_group, total // (n_inner * n_group))
    amps = lax.all_to_all(shaped, "group", split_axis=2, concat_axis=2, tiled=True).reshape(
        2, total
    )
    amps = apply_gate(amps, gates[4], upper - inner_bits)
    amps = apply_gate(amps, gates[5], 0)
    amps = apply_gate(amps, gates[6], upper)
    amps = apply_gate(amps, gates[7], upper // 2)
    shaped = amps.reshape(2, n_inner, n_group, total // (n_inner * n_group))
    shaped = lax.all_to_all(shaped, "group", split_axis=2, concat_axis=2, tiled=True)
    shaped = lax.all_to_all(shaped, "inner", split_axis=1, concat_axis=1, tiled=True)
    return shaped.reshape(2, total)


F32 = jnp.float32
BF16 = jnp.bfloat16


def split(value):
    high = value.astype(BF16)
    return high, (value - high.astype(F32)).astype(BF16)


def dot3(left, right, transposed=False):
    dims = (((1,), (1 if transposed else 0,)), ((), ()))
    mul = functools.partial(lax.dot_general, dimension_numbers=dims, preferred_element_type=F32)
    (lh, ll), (rh, rl) = left, right
    return mul(lh, rh) + (mul(lh, rl) + mul(ll, rh))


def exchange(x, axis, pairs):
    lane = lax.broadcasted_iota(jnp.int32, (1, x.shape[-1]), 1)
    for lane_bit, bit in pairs:
        shift = 1 << lane_bit
        upper = ((lane >> lane_bit) & 1) == 1
        shape = x.shape
        y = x.reshape(shape[:axis] + (shape[axis] >> (bit + 1), 2, 1 << bit) + shape[axis + 1 :])
        cut = (slice(None),) * (axis + 1)
        a, b = y[cut + (0,)], y[cut + (1,)]
        rows = a.reshape(-1, shape[-1])
        ra = pltpu.roll(rows, shape[-1] - shift, 1).reshape(a.shape)
        rb = pltpu.roll(b.reshape(-1, shape[-1]), shift, 1).reshape(a.shape)
        first = jnp.where(upper, rb, a)
        second = jnp.where(upper, b, ra)
        x = jnp.stack([first, second], axis + 1).reshape(shape)
    return x


def order_index(index, dims, order):
    bits = [d.bit_length() - 1 for d in dims]
    source, low = 0, 0
    for axis in reversed(order):
        digit = (index >> low) & (dims[axis] - 1)
        source = source + (digit << sum(bits[axis + 1 :]))
        low += bits[axis]
    return source


def kernel(
    n_group,
    n_inner,
    x_hbm,
    g_hbm,
    o_ref,
    x_ref,
    g_ref,
    send1,
    recv1,
    send2,
    recv2,
    tmp,
    weights,
    ssem,
    rsem,
    lsem,
):
    devices = n_group * n_inner
    size = x_ref.shape[1]
    wide = 2 * size
    mid = x_ref.shape[0] // wide
    rest = size // devices
    low = size // devices
    half = size // n_group // low
    seven = mid // half
    chunks = 2
    sub = 2 * low
    group, inner = lax.axis_index("group"), lax.axis_index("inner")
    me = group * n_inner + inner

    def peer(step):
        other = lax.rem(me + step, devices)
        return other, (other // n_inner, lax.rem(other, n_inner))

    load_g = pltpu.make_async_copy(g_hbm, g_ref, lsem.at[0])
    load_x = pltpu.make_async_copy(x_hbm, x_ref, lsem.at[1])
    load_g.start()
    load_x.start()
    barrier = pltpu.get_barrier_semaphore()

    @pl.loop(1, devices)
    def _(step):
        pl.semaphore_signal(
            barrier, inc=1, device_id=peer(step)[1], device_id_type=pl.DeviceIdType.MESH
        )

    def gate(k):
        re, im = g_ref[k, 0], g_ref[k, 1]
        return jnp.concatenate(
            [jnp.concatenate([re, -im], axis=1), jnp.concatenate([im, re], axis=1)], axis=0
        )

    def place(k, matrix, order, columns=True):
        for part, piece in enumerate(split(matrix)):
            piece = select(order, piece)
            if columns:
                piece = select(order, piece, False)
            weights[k, part] = piece.astype(BF16)

    def select(order, piece, rows=True):
        shape = (wide, wide)
        source = order_index(lax.broadcasted_iota(jnp.int32, shape, 0), *order)
        hit = source == lax.broadcasted_iota(jnp.int32, shape, 1)
        ones = jnp.where(hit, 1.0, 0.0).astype(BF16)
        left, right = (ones, piece) if rows else (piece.astype(BF16), ones)
        dims = (((1,), (0 if rows else 1,)), ((), ()))
        return lax.dot_general(left, right, dims, preferred_element_type=F32)

    def weight(k):
        return weights[k, 0], weights[k, 1]

    def copies(swap, chunk, step, source, landing):
        other, where = peer(step)
        return pltpu.make_async_remote_copy(
            src_ref=source.at[chunk, other],
            dst_ref=landing.at[chunk, me],
            send_sem=ssem.at[swap, chunk, step],
            recv_sem=rsem.at[swap, chunk, step],
            device_id=where,
            device_id_type=pl.DeviceIdType.MESH,
        )

    def start(swap, chunk, source, landing):
        @pl.loop(1, devices)
        def _(step):
            copies(swap, chunk, step, source, landing).start()

        landing[chunk, me] = source[chunk, me]

    def finish(swap, chunk, source, landing):
        @pl.loop(1, devices)
        def _(step):
            copies(swap, chunk, step, source, landing).wait()

    load_g.wait()
    place(0, gate(1), ((2, chunks, n_inner // chunks, n_group, low), (0, 1, 4, 2, 3)), False)
    merged = dot3(split(gate(3)), split(gate(0)))
    merged = dot3(split(gate(5)), split(merged))
    place(1, merged, ((2, rest, devices), (2, 0, 1)), False)

    load_x.wait()

    cols = [
        jnp.concatenate(
            [x_ref[pl.ds(2 * q + c, size, stride=2 * mid), :] for c in range(2)], axis=0
        )
        for q in range(mid)
    ]
    y = dot3(weight(0), split(jnp.concatenate(cols, axis=1)))
    run = size // (chunks * low)
    tiles = [
        y[:, q * size : (q + 1) * size].reshape(2, chunks, low, run, size) for q in range(mid)
    ]
    y = jnp.stack(tiles, 3)
    y = y.reshape(2, chunks, low * size, size)
    pl.semaphore_wait(barrier, devices - 1)
    for chunk in range(chunks):
        rows = jnp.concatenate([y[0, chunk], y[1, chunk]], axis=1)
        z = dot3(weight(1), split(rows), True)
        for w in range(low):
            piece = z[:, w * size : (w + 1) * size].reshape(devices, 2 * rest, size)
            send1[chunk, :, w * 2 * rest : (w + 1) * 2 * rest, :] = piece
        start(0, chunk, send1, recv1)

    place(2, gate(2), ((2, n_inner, n_group, low), (2, 1, 3, 0)))
    place(3, gate(4), ((2, n_group, low, half), (3, 1, 2, 0)))
    place(4, gate(6), ((2, n_inner, n_group, low), (2, 1, 3, 0)))
    place(5, gate(7), ((2, low, half, seven, rest), (2, 4, 3, 1, 0)))

    bits_t = range(n_group.bit_length() - 1)
    lane_bits = size.bit_length() - 1
    bits_r = range(rest.bit_length() - 1)
    top = lane_bits - len(bits_r)
    pair_tu = [(k, k) for k in bits_t]
    pair_er = [(top + k, k) for k in bits_r]
    pair_t7 = [(lane_bits - len(bits_t) + k, k) for k in bits_t]

    def apply(k, x, axis):
        parts = x.shape[axis]
        picked = [lax.index_in_dim(x, i, axis, keepdims=False) for i in range(parts)]
        kept = picked[0].shape
        flat = jnp.concatenate([p.reshape(wide, size) for p in picked], axis=1)
        out = dot3(weight(k), split(flat))
        pieces = [out[:, i * size : (i + 1) * size].reshape(kept) for i in range(parts)]
        return jnp.stack(pieces, axis)

    for chunk in range(chunks):
        finish(0, chunk, send1, recv1)
        flat = recv1.at[chunk].reshape(devices * sub * rest, size)
        x = jnp.stack([flat[pl.ds(r, devices * sub, stride=rest), :] for r in range(rest)], 0)
        x = x.reshape(rest, n_group, n_inner, sub, size)
        x = exchange(x, 1, pair_tu)
        x = apply(2, x, 0)
        x = exchange(x, 1, pair_tu)
        x = exchange(x, 0, pair_er)
        x = apply(3, x, 2)
        x = apply(4, x, 0)
        x = exchange(x, 1, pair_t7)
        x = apply(5, x, 2)
        x = exchange(x, 1, pair_t7)
        x = x.reshape(half, devices, sub, size)
        for e in range(half):
            send2[chunk, :, e * sub : (e + 1) * sub, :] = x[e]
        start(1, chunk, send2, recv2)

    span = x_ref.shape[0] // chunks
    for chunk in range(chunks):
        finish(1, chunk, send2, recv2)
        x = recv2[chunk].reshape(devices, half, sub, size)
        x = exchange(x, 0, [(k, k) for k in range(top)])
        x = x.reshape(seven, devices // seven, half, sub, size)
        for p in range(seven):
            for e in range(half):
                tmp[:, (e * seven + p) * sub : (e * seven + p + 1) * sub, :] = x[p, :, e]
        flat = tmp.reshape(devices // seven * mid * sub, size)
        for hi in range(devices // seven):
            for w in range(low):
                for c in range(2):
                    rows = flat[pl.ds(hi * mid * sub + w * 2 + c, mid, stride=sub), :]
                    at = chunk * span + (hi * low + w) * 2 * mid + c
                    o_ref[pl.ds(at, mid, stride=2), :] = rows


def fast_body(state, gates, n_group, n_inner):
    size = gates.shape[-1]
    total = state.shape[1]
    devices = n_group * n_inner
    low = size // devices
    half = size // n_group // low
    mid = total // size // size
    seven = mid // half
    wide = 2 * size
    x = state.reshape(2, total // size, size).transpose(1, 0, 2).reshape(-1, size)
    chunk = (2, devices, x.shape[0] // 2 // devices, size)
    vmem = pl.BlockSpec(memory_space=pltpu.VMEM)
    out = pl.pallas_call(
        functools.partial(kernel, n_group, n_inner),
        out_shape=jax.ShapeDtypeStruct(x.shape, F32),
        in_specs=[pl.BlockSpec(memory_space=pltpu.HBM)] * 2,
        out_specs=vmem,
        scratch_shapes=[
            pltpu.VMEM(x.shape, F32),
            pltpu.VMEM(gates.shape, F32),
            pltpu.VMEM(chunk, F32),
            pltpu.VMEM(chunk, F32),
            pltpu.VMEM(chunk, F32),
            pltpu.VMEM(chunk, F32),
            pltpu.VMEM((devices // seven, mid * 2 * low, size), F32),
            pltpu.VMEM((6, 2, wide, wide), BF16),
            pltpu.SemaphoreType.DMA((2, 2, devices)),
            pltpu.SemaphoreType.DMA((2, 2, devices)),
            pltpu.SemaphoreType.DMA((2,)),
        ],
        compiler_params=pltpu.CompilerParams(
            collective_id=0, has_side_effects=True, vmem_limit_bytes=52 << 20
        ),
    )(x, gates)
    return out.reshape(total // size, 2, size).transpose(1, 0, 2).reshape(2, total)


def solution(mesh):
    n_inner, n_group = mesh.shape["inner"], mesh.shape["group"]

    def body(state, gates):
        size, total = gates.shape[-1], state.shape[1]
        gate_bits, local_bits = size.bit_length() - 1, total.bit_length() - 1
        inner_bits = n_inner.bit_length() - 1
        device_bits = inner_bits + n_group.bit_length() - 1
        upper = local_bits - gate_bits
        fits = (
            device_bits == upper // 2
            and upper // 2 + gate_bits == local_bits - device_bits
            and upper - inner_bits >= gate_bits
        )
        if fits:
            return fast_body(state, gates, n_group, n_inner)
        return general_body(state, gates)

    in_specs = (P(None, ("group", "inner")), P())
    out_specs = P(None, ("group", "inner"))
    return jax.shard_map(body, mesh=mesh, in_specs=in_specs, out_specs=out_specs, check_vma=False)
```

```python
import functools

import jax
import jax.numpy as jnp
from jax import lax
from jax.experimental import pallas as pl
from jax.experimental.pallas import tpu as pltpu
from jax.sharding import PartitionSpec as P


def blocked(mixer):
    real_part = mixer[0]
    imag_part = mixer[1]
    return jnp.stack(
        [jnp.stack([real_part, -imag_part], 1), jnp.stack([imag_part, real_part], 1)], 0
    )


def apply_gate(state, mixer, start):
    size = mixer.shape[-1]
    total = state.shape[1]
    block = blocked(mixer)
    if start == 0:
        view = state.reshape(2, total // size, size)
        result = jnp.einsum("ckdj,daj->cak", block, view, precision=lax.Precision.HIGHEST)
    else:
        view = state.reshape(2, total // (size << start), size, 1 << start)
        result = jnp.einsum("ckdj,dajb->cakb", block, view, precision=lax.Precision.HIGHEST)
    return result.reshape(2, total)


def general_body(state, gates):
    n_inner = lax.axis_size("inner")
    n_group = lax.axis_size("group")
    total = state.shape[1]
    size = gates.shape[-1]
    local_bits = total.bit_length() - 1
    gate_bits = size.bit_length() - 1
    inner_bits = n_inner.bit_length() - 1
    upper = local_bits - gate_bits
    amps = apply_gate(state, gates[0], 0)
    amps = apply_gate(amps, gates[1], upper)
    low_gate = gates[3]
    shaped = amps.reshape(2, n_inner, total // (n_inner * size), size)
    pieces = lax.all_to_all(shaped, "inner", split_axis=1, concat_axis=1, tiled=True)
    amps = apply_gate(pieces.reshape(2, -1), low_gate, 0).reshape(pieces.shape).reshape(2, total)
    amps = apply_gate(amps, gates[2], upper)
    shaped = amps.reshape(2, n_inner, n_group, total // (n_inner * n_group))
    amps = lax.all_to_all(shaped, "group", split_axis=2, concat_axis=2, tiled=True).reshape(
        2, total
    )
    amps = apply_gate(amps, gates[4], upper - inner_bits)
    amps = apply_gate(amps, gates[5], 0)
    amps = apply_gate(amps, gates[6], upper)
    amps = apply_gate(amps, gates[7], upper // 2)
    shaped = amps.reshape(2, n_inner, n_group, total // (n_inner * n_group))
    shaped = lax.all_to_all(shaped, "group", split_axis=2, concat_axis=2, tiled=True)
    shaped = lax.all_to_all(shaped, "inner", split_axis=1, concat_axis=1, tiled=True)
    return shaped.reshape(2, total)


F32 = jnp.float32
BF16 = jnp.bfloat16


def split(value):
    high = value.astype(BF16)
    return high, (value - high.astype(F32)).astype(BF16)


def dot3(left, right, transposed=False):
    dims = (((1,), (1 if transposed else 0,)), ((), ()))
    mul = functools.partial(lax.dot_general, dimension_numbers=dims, preferred_element_type=F32)
    (lh, ll), (rh, rl) = left, right
    return mul(lh, rh) + (mul(lh, rl) + mul(ll, rh))


def exchange(x, axis, pairs):
    lane = lax.broadcasted_iota(jnp.int32, (1, x.shape[-1]), 1)
    for lane_bit, bit in pairs:
        shift = 1 << lane_bit
        upper = ((lane >> lane_bit) & 1) == 1
        shape = x.shape
        y = x.reshape(shape[:axis] + (shape[axis] >> (bit + 1), 2, 1 << bit) + shape[axis + 1 :])
        cut = (slice(None),) * (axis + 1)
        a, b = y[cut + (0,)], y[cut + (1,)]
        rows = a.reshape(-1, shape[-1])
        ra = pltpu.roll(rows, shape[-1] - shift, 1).reshape(a.shape)
        rb = pltpu.roll(b.reshape(-1, shape[-1]), shift, 1).reshape(a.shape)
        first = jnp.where(upper, rb, a)
        second = jnp.where(upper, b, ra)
        x = jnp.stack([first, second], axis + 1).reshape(shape)
    return x


def order_index(index, dims, order):
    bits = [d.bit_length() - 1 for d in dims]
    source, low = 0, 0
    for axis in reversed(order):
        digit = (index >> low) & (dims[axis] - 1)
        source = source + (digit << sum(bits[axis + 1 :]))
        low += bits[axis]
    return source


def kernel(
    n_group,
    n_inner,
    x_hbm,
    g_hbm,
    o_ref,
    x_ref,
    g_ref,
    send1,
    recv1,
    send2,
    recv2,
    tmp,
    weights,
    ssem,
    rsem,
    lsem,
):
    devices = n_group * n_inner
    size = x_ref.shape[1]
    wide = 2 * size
    mid = x_ref.shape[0] // wide
    rest = size // devices
    low = size // devices
    half = size // n_group // low
    seven = mid // half
    chunks = 2
    sub = 2 * low
    group, inner = lax.axis_index("group"), lax.axis_index("inner")
    me = group * n_inner + inner

    def peer(step):
        other = lax.rem(me + step, devices)
        return other, (other // n_inner, lax.rem(other, n_inner))

    load_g = pltpu.make_async_copy(g_hbm, g_ref, lsem.at[0])
    load_x = pltpu.make_async_copy(x_hbm, x_ref, lsem.at[1])
    load_g.start()
    load_x.start()
    barrier = pltpu.get_barrier_semaphore()

    @pl.loop(1, devices)
    def _(step):
        pl.semaphore_signal(
            barrier, inc=1, device_id=peer(step)[1], device_id_type=pl.DeviceIdType.MESH
        )

    def gate(k):
        re, im = g_ref[k, 0], g_ref[k, 1]
        return jnp.concatenate(
            [jnp.concatenate([re, -im], axis=1), jnp.concatenate([im, re], axis=1)], axis=0
        )

    def place(k, matrix, order, columns=True):
        for part, piece in enumerate(split(matrix)):
            piece = select(order, piece)
            if columns:
                piece = select(order, piece, False)
            weights[k, part] = piece.astype(BF16)

    def select(order, piece, rows=True):
        shape = (wide, wide)
        source = order_index(lax.broadcasted_iota(jnp.int32, shape, 0), *order)
        hit = source == lax.broadcasted_iota(jnp.int32, shape, 1)
        ones = jnp.where(hit, 1.0, 0.0).astype(BF16)
        left, right = (ones, piece) if rows else (piece.astype(BF16), ones)
        dims = (((1,), (0 if rows else 1,)), ((), ()))
        return lax.dot_general(left, right, dims, preferred_element_type=F32)

    def weight(k):
        return weights[k, 0], weights[k, 1]

    def copies(swap, chunk, step, source, landing):
        other, where = peer(step)
        return pltpu.make_async_remote_copy(
            src_ref=source.at[chunk, other],
            dst_ref=landing.at[chunk, me],
            send_sem=ssem.at[swap, chunk, step],
            recv_sem=rsem.at[swap, chunk, step],
            device_id=where,
            device_id_type=pl.DeviceIdType.MESH,
        )

    def start(swap, chunk, source, landing):
        @pl.loop(1, devices)
        def _(step):
            copies(swap, chunk, step, source, landing).start()

        landing[chunk, me] = source[chunk, me]

    def finish(swap, chunk, source, landing):
        @pl.loop(1, devices)
        def _(step):
            copies(swap, chunk, step, source, landing).wait()

    load_g.wait()
    place(0, gate(1), ((2, chunks, n_inner // chunks, n_group, low), (0, 1, 4, 2, 3)), False)
    merged = dot3(split(gate(3)), split(gate(0)))
    merged = dot3(split(gate(5)), split(merged))
    place(1, merged, ((2, rest, devices), (2, 0, 1)), False)

    load_x.wait()

    cols = [
        jnp.concatenate(
            [x_ref[pl.ds(2 * q + c, size, stride=2 * mid), :] for c in range(2)], axis=0
        )
        for q in range(mid)
    ]
    y = dot3(weight(0), split(jnp.concatenate(cols, axis=1)))
    run = size // (chunks * low)
    tiles = [
        y[:, q * size : (q + 1) * size].reshape(2, chunks, low, run, size) for q in range(mid)
    ]
    y = jnp.stack(tiles, 3)
    y = y.reshape(2, chunks, low * size, size)
    for chunk in range(chunks):
        rows = jnp.concatenate([y[0, chunk], y[1, chunk]], axis=1)
        z = dot3(weight(1), split(rows), True)
        for w in range(low):
            piece = z[:, w * size : (w + 1) * size].reshape(devices, 2 * rest, size)
            send1[chunk, :, w * 2 * rest : (w + 1) * 2 * rest, :] = piece
        if chunk == 0:
            pl.semaphore_wait(barrier, devices - 1)
        start(0, chunk, send1, recv1)

    place(2, gate(2), ((2, n_inner, n_group, low), (2, 1, 3, 0)))
    place(3, gate(4), ((2, n_group, low, half), (3, 1, 2, 0)))
    place(4, gate(6), ((2, n_inner, n_group, low), (2, 1, 3, 0)))
    place(5, gate(7), ((2, low, half, seven, rest), (2, 4, 3, 1, 0)))

    bits_t = range(n_group.bit_length() - 1)
    lane_bits = size.bit_length() - 1
    bits_r = range(rest.bit_length() - 1)
    top = lane_bits - len(bits_r)
    pair_tu = [(k, k) for k in bits_t]
    pair_er = [(top + k, k) for k in bits_r]
    pair_t7 = [(lane_bits - len(bits_t) + k, k) for k in bits_t]

    def apply(k, x, axis):
        parts = x.shape[axis]
        picked = [lax.index_in_dim(x, i, axis, keepdims=False) for i in range(parts)]
        kept = picked[0].shape
        flat = jnp.concatenate([p.reshape(wide, size) for p in picked], axis=1)
        out = dot3(weight(k), split(flat))
        pieces = [out[:, i * size : (i + 1) * size].reshape(kept) for i in range(parts)]
        return jnp.stack(pieces, axis)

    for chunk in range(chunks):
        finish(0, chunk, send1, recv1)
        flat = recv1.at[chunk].reshape(devices * sub * rest, size)
        x = jnp.stack([flat[pl.ds(r, devices * sub, stride=rest), :] for r in range(rest)], 0)
        x = x.reshape(rest, n_group, n_inner, sub, size)
        x = exchange(x, 1, pair_tu)
        x = apply(2, x, 0)
        x = exchange(x, 1, pair_tu)
        x = exchange(x, 0, pair_er)
        x = apply(3, x, 2)
        x = apply(4, x, 0)
        x = exchange(x, 1, pair_t7)
        x = apply(5, x, 2)
        x = exchange(x, 1, pair_t7)
        x = x.reshape(half, devices, sub, size)
        for e in range(half):
            send2[chunk, :, e * sub : (e + 1) * sub, :] = x[e]
        start(1, chunk, send2, recv2)

    span = x_ref.shape[0] // chunks
    for chunk in range(chunks):
        finish(1, chunk, send2, recv2)
        x = recv2[chunk].reshape(devices, half, sub, size)
        x = exchange(x, 0, [(k, k) for k in range(top)])
        x = x.reshape(seven, devices // seven, half, sub, size)
        for p in range(seven):
            for e in range(half):
                tmp[:, (e * seven + p) * sub : (e * seven + p + 1) * sub, :] = x[p, :, e]
        flat = tmp.reshape(devices // seven * mid * sub, size)
        for hi in range(devices // seven):
            for w in range(low):
                for c in range(2):
                    rows = flat[pl.ds(hi * mid * sub + w * 2 + c, mid, stride=sub), :]
                    at = chunk * span + (hi * low + w) * 2 * mid + c
                    o_ref[pl.ds(at, mid, stride=2), :] = rows


def fast_body(state, gates, n_group, n_inner):
    size = gates.shape[-1]
    total = state.shape[1]
    devices = n_group * n_inner
    low = size // devices
    half = size // n_group // low
    mid = total // size // size
    seven = mid // half
    wide = 2 * size
    x = state.reshape(2, total // size, size).transpose(1, 0, 2).reshape(-1, size)
    chunk = (2, devices, x.shape[0] // 2 // devices, size)
    vmem = pl.BlockSpec(memory_space=pltpu.VMEM)
    out = pl.pallas_call(
        functools.partial(kernel, n_group, n_inner),
        out_shape=jax.ShapeDtypeStruct(x.shape, F32),
        in_specs=[pl.BlockSpec(memory_space=pltpu.HBM)] * 2,
        out_specs=vmem,
        scratch_shapes=[
            pltpu.VMEM(x.shape, F32),
            pltpu.VMEM(gates.shape, F32),
            pltpu.VMEM(chunk, F32),
            pltpu.VMEM(chunk, F32),
            pltpu.VMEM(chunk, F32),
            pltpu.VMEM(chunk, F32),
            pltpu.VMEM((devices // seven, mid * 2 * low, size), F32),
            pltpu.VMEM((6, 2, wide, wide), BF16),
            pltpu.SemaphoreType.DMA((2, 2, devices)),
            pltpu.SemaphoreType.DMA((2, 2, devices)),
            pltpu.SemaphoreType.DMA((2,)),
        ],
        compiler_params=pltpu.CompilerParams(
            collective_id=0, has_side_effects=True, vmem_limit_bytes=52 << 20
        ),
    )(x, gates)
    return out.reshape(total // size, 2, size).transpose(1, 0, 2).reshape(2, total)


def solution(mesh):
    n_inner, n_group = mesh.shape["inner"], mesh.shape["group"]

    def body(state, gates):
        size, total = gates.shape[-1], state.shape[1]
        gate_bits, local_bits = size.bit_length() - 1, total.bit_length() - 1
        inner_bits = n_inner.bit_length() - 1
        device_bits = inner_bits + n_group.bit_length() - 1
        upper = local_bits - gate_bits
        fits = (
            device_bits == upper // 2
            and upper // 2 + gate_bits == local_bits - device_bits
            and upper - inner_bits >= gate_bits
        )
        if fits:
            return fast_body(state, gates, n_group, n_inner)
        return general_body(state, gates)

    in_specs = (P(None, ("group", "inner")), P())
    out_specs = P(None, ("group", "inner"))
    return jax.shard_map(body, mesh=mesh, in_specs=in_specs, out_specs=out_specs, check_vma=False)
```
